32 devices in a mesh: pb: 4 (over y, core), ma: 8 (over z, x).
Axes of the slice: x: 2, y: 2, z: 4, core: 2. Of those that a mesh axis runs over, the one named last changes fastest.
Arguments:
- queries: bfloat16 [1, 1024, 2048], P(None, ('pb', 'ma')), may hold values from -6 to 6
- map_descriptors: bfloat16 [8192, 2048], P('ma', 'pb'), may hold values from -0.125 to 0.125
- slopes: int32 [8], replicated, may hold values from 0 to 15, as said below
Outputs:
- best: float32 [1, 1024, 8192], P(None, 'pb', 'ma')
The draws below stay inside these ranges and needn't reach their ends.
Inputs may be any that keep to these rules, and one draw needn't show every extreme that they name: `slopes`: 8 distinct velocities; the largest is exactly 15.
All inputs are finite; a program needn't handle non-finite values.
Results may differ from the reference program's by a relative error of at most 0.0003.
Values may be sent and summed in bfloat16 or wider, within the bound.
A program may use at most 64 MiB of HBM per device.

```python
import math
import jax
import jax.numpy as jnp
from jax import lax

D = 2048
SESS = 1
SEQ = 20
RAD = 10
VMAX = 15
NSLOPE = 8
SPAN = 285
NQ = 1024
NM = 8192


def draw_slopes(key, part):
    order = jax.random.permutation(key, VMAX + 1)[:NSLOPE]
    largest = jnp.max(order)
    return jnp.where(order == largest, VMAX, order).astype(jnp.int32)


def steps_of(key, dims, cuts, smallest, high):
    factor_of = 1.0
    for axis_at, shards_of in cuts:
        heights = jax.random.uniform(jax.random.fold_in(jax.random.fold_in(key, 6), axis_at), (shards_of,), jnp.float32, smallest / len(cuts), high / len(cuts))
        factor_of = factor_of * jnp.repeat(jnp.exp(heights), dims[axis_at] // shards_of).reshape((-1,) + (1,) * (len(dims) - 1 - axis_at))
    return factor_of


def gaussian(key, dims, deviation, bound, cuts=(), held_as=jnp.bfloat16):
    result = jax.random.normal(key, dims, jnp.float32) * deviation
    if len(cuts) > 0:
        result = steps_of(key, dims, cuts, -0.22, 0.18) * result
    return jnp.clip(result, min=-bound, max=bound).astype(held_as)


def setup_inputs(seed: int = 0) -> dict:
    streams_of = jax.random.split(jax.random.key(seed), 4)
    return {
        "queries": gaussian(streams_of[0], (SESS, NQ, D), 1.0, 6.0, ((1, 32),)),
        "map_descriptors": gaussian(streams_of[1], (NM, D), D ** -0.5, 0.125, ((0, 8), (1, 4))),
        "slopes": draw_slopes(jax.random.fold_in(streams_of[3], 71), 0),
    }


def reference(queries, map_descriptors, slopes):

    def one_traversal(query_rows):
        scores = lax.dot_general(query_rows, map_descriptors, (((1,), (1,)), ((), ())), preferred_element_type=jnp.float32)
        padded = jnp.pad(scores, ((0, 0), (RAD, RAD)))
        running = jnp.zeros(scores.shape, jnp.float32)
        squares = jnp.zeros(scores.shape, jnp.float32)
        for offset in range(2 * RAD + 1):
            window = padded[:, offset:offset + NM]
            running = running + window
            squares = squares + window * window
        average = running / (2 * RAD + 1)
        spread = squares / (2 * RAD + 1) - average * average
        normal = (scores - average) / jnp.sqrt(spread + 1.0)
        normal_pad = jnp.pad(normal, ((SEQ - 1, 0), (SPAN, 0)))

        def per_slope(best_val, velocity):
            summed = jnp.zeros((NQ, NM), jnp.float32)
            for lag_step in range(SEQ):
                row_at = jnp.asarray(SEQ - 1 - lag_step, jnp.int32)
                col_at = (SPAN - lag_step * velocity).astype(jnp.int32)
                summed = summed + lax.dynamic_slice(normal_pad, (row_at, col_at), (NQ, NM))
            return (jnp.maximum(best_val, summed), None)
        start_best = jnp.full((NQ, NM), -jnp.inf, jnp.float32)
        best_val, unused = lax.scan(per_slope, start_best, slopes)
        return best_val / math.sqrt(SEQ)
    return lax.map(one_traversal, queries)
```

```python
import math

import jax
import jax.numpy as jnp
from jax import lax
from jax.experimental import pallas as pl
from jax.experimental.pallas import tpu as pltpu
from jax.sharding import PartitionSpec as P

MESH = pl.DeviceIdType.MESH
SEQ = 20
RAD = 10
LEAD = 32
LEFT = 384
RIGHT = 128
LANES = 128
CORES = 2


def remote(src, dst, send, recv, where):
    return pltpu.make_async_remote_copy(
        src_ref=src,
        dst_ref=dst,
        send_sem=send,
        recv_sem=recv,
        device_id=where,
        device_id_type=MESH,
    )


def score_kernel(
    npb,
    nma,
    chunks,
    q_ref,
    m_ref,
    out_ref,
    q_all,
    q_lead,
    m_all,
    scores,
    left,
    right,
    local_sem,
    q_send,
    q_recv,
    lead_sem,
    m_send,
    m_recv,
    halo_send,
    halo_recv,
):
    pb, ma = lax.axis_index("pb"), lax.axis_index("ma")
    pair, across = npb // CORES, nma // 2
    row, core = pb // CORES, pb % CORES
    z, x = ma // 2, ma % 2
    mate = row * CORES + 1 - core
    twin = z * 2 + 1 - x
    rows_other = [((row + i) % pair) * CORES + core for i in range(1, pair)]
    rows_from = [((row + pair - i) % pair) * CORES + core for i in range(1, pair)]
    z_other = [((z + i) % across) * 2 + x for i in range(1, across)]
    z_from = [((z + across - i) % across) * 2 + x for i in range(1, across)]
    has_up, has_down = pb > 0, pb < npb - 1
    has_left, has_right = ma > 0, ma < nma - 1

    load_q = pltpu.make_async_copy(q_ref.at[0], q_all.at[ma], local_sem.at[0])
    load_q.start()
    load_m = pltpu.make_async_copy(m_ref, m_all.at[pb], local_sem.at[1])
    load_m.start()

    barrier = pltpu.get_barrier_semaphore()

    def greet(where):
        pl.semaphore_signal(barrier, inc=1, device_id=where, device_id_type=MESH)

    greet({"pb": mate})
    greet({"ma": twin})
    for other in rows_other:
        greet({"pb": other})
    for other in z_other:
        greet({"ma": other})
    for test, where in (
        (has_up, {"pb": pb - 1}),
        (has_down, {"pb": pb + 1}),
        (has_left, {"ma": ma - 1}),
        (has_right, {"ma": ma + 1}),
    ):

        @pl.when(test)
        def _():
            greet(where)

    edges = sum(
        jnp.where(test, 1, 0) for test in (has_up, has_down, has_left, has_right)
    )
    pl.semaphore_wait(barrier, pair + across + edges)

    load_q.wait()
    q_to_z = [
        remote(q_all.at[ma], q_all.at[ma], q_send.at[i], q_recv.at[i], {"ma": other})
        for i, other in enumerate(z_other)
    ]
    for copy in q_to_z:
        copy.start()
    first = across - 1
    q_to_x = [
        remote(
            q_all.at[ma], q_all.at[ma], q_send.at[first], q_recv.at[first], {"ma": twin}
        )
    ]
    q_to_x[0].start()

    load_m.wait()
    m_count = m_ref.shape[0]
    step = m_count // chunks
    order = list(range(chunks - 1, chunks // 2 - 1, -1)) + list(range(chunks // 2))

    def piece(slot, chunk):
        return m_all.at[slot, pl.ds(chunk * step, step)]

    m_to_row, m_to_mate = {}, {}
    for chunk in order:
        for i, other in enumerate(rows_other):
            at = i * chunks + chunk
            m_to_row[i, chunk] = remote(
                piece(pb, chunk), piece(pb, chunk), m_send.at[at], m_recv.at[at], {"pb": other}
            )
            m_to_row[i, chunk].start()
    for chunk in order:
        at = (pair - 1) * chunks + chunk
        m_to_mate[-1, chunk] = remote(
            piece(pb, chunk), piece(pb, chunk), m_send.at[at], m_recv.at[at], {"pb": mate}
        )
        m_to_mate[-1, chunk].start()

    for i, source in enumerate(z_from):
        q_to_z[i].wait_recv()
        at = across + i
        copy = remote(
            q_all.at[source], q_all.at[source], q_send.at[at], q_recv.at[at], {"ma": twin}
        )
        copy.start()
        q_to_x.append(copy)
    for copy in q_to_x:
        copy.wait_recv()

    held = q_lead.shape[0]
    lead = remote(
        q_all.at[pl.ds(nma - held, held)], q_lead, lead_sem.at[0], lead_sem.at[1], {"pb": pb + 1}
    )

    @pl.when(has_down)
    def _():
        lead.start()

    @pl.when(pb == 0)
    def _():
        q_lead[...] = jnp.zeros_like(q_lead)

    @pl.when(ma == 0)
    def _():
        left[...] = jnp.zeros_like(left)

    @pl.when(ma == nma - 1)
    def _():
        right[...] = jnp.zeros_like(right)

    def flat(ref):
        count, each, width = ref.shape
        if each % 16 == 0:
            return ref[...].reshape(count * each, width)
        return ref[...].astype(jnp.float32).reshape(count * each, width).astype(ref.dtype)

    to_right = remote(
        scores.at[:, pl.ds(m_count - LEFT, LEFT)],
        left,
        halo_send.at[0],
        halo_recv.at[0],
        {"ma": ma + 1},
    )
    to_left = remote(
        scores.at[:, pl.ds(0, RIGHT)],
        right,
        halo_send.at[1],
        halo_recv.at[1],
        {"ma": ma - 1},
    )
    done = set()
    for number, chunk in enumerate(order):
        for i, source in enumerate(rows_from):
            m_to_row[i, chunk].wait_recv()
            at = (pair + i) * chunks + chunk
            m_to_mate[i, chunk] = remote(
                piece(source, chunk), piece(source, chunk), m_send.at[at], m_recv.at[at], {"pb": mate}
            )
            m_to_mate[i, chunk].start()
        for i in range(-1, pair - 1):
            m_to_mate[i, chunk].wait_recv()
        if number == 0:

            @pl.when(has_up)
            def _():
                lead.wait_recv()

        k = m_ref.shape[1]
        for queries, at in ((q_lead, 0), (q_all, LEAD)):
            total = None
            block = flat(queries)
            for slot in range(npb):
                part = lax.dot_general(
                    block[:, slot * k : (slot + 1) * k],
                    m_all[slot, pl.ds(chunk * step, step), :],
                    (((1,), (1,)), ((), ())),
                    preferred_element_type=jnp.float32,
                )
                total = part if total is None else total + part
            scores[pl.ds(at, block.shape[0]), pl.ds(chunk * step, step)] = total
        before = set(done)
        done.update(range(chunk * step, (chunk + 1) * step, LANES))
        right_part = set(range(m_count - LEFT, m_count, LANES))
        left_part = set(range(0, RIGHT, LANES))
        if right_part <= done and not right_part <= before:

            @pl.when(has_right)
            def _():
                to_right.start()

        if left_part <= done and not left_part <= before:

            @pl.when(has_left)
            def _():
                to_left.start()

    out_ref[:, pl.ds(LEFT, m_count)] = scores[...]

    @pl.when(has_left)
    def _():
        to_right.wait_recv()

    out_ref[:, pl.ds(0, LEFT)] = left[...]

    @pl.when(has_right)
    def _():
        to_left.wait_recv()

    out_ref[:, pl.ds(LEFT + m_count, RIGHT)] = right[...]

    for copy in q_to_z + q_to_x + list(m_to_row.values()) + list(m_to_mate.values()):
        copy.wait_send()

    @pl.when(has_down)
    def _():
        lead.wait_send()

    @pl.when(has_right)
    def _():
        to_right.wait_send()

    @pl.when(has_left)
    def _():
        to_left.wait_send()


def score_tile(queries, map_descriptors, npb, nma):
    each, width = queries.shape[1:]
    m_count, k = map_descriptors.shape
    q_count = each * nma
    chunks = 4
    held = LEAD // each
    pair, across = npb // CORES, nma // 2
    dma = pltpu.SemaphoreType.DMA
    return pl.pallas_call(
        lambda *refs: score_kernel(npb, nma, chunks, *refs),
        out_shape=jax.ShapeDtypeStruct(
            (LEAD + q_count, LEFT + m_count + RIGHT), jnp.float32
        ),
        in_specs=[pl.BlockSpec(memory_space=pl.ANY)] * 2,
        out_specs=pl.BlockSpec(memory_space=pltpu.VMEM),
        scratch_shapes=[
            pltpu.VMEM((nma, each, width), jnp.bfloat16),
            pltpu.VMEM((held, each, width), jnp.bfloat16),
            pltpu.VMEM((npb, m_count, k), jnp.bfloat16),
            pltpu.VMEM((LEAD + q_count, m_count), jnp.float32),
            pltpu.VMEM((LEAD + q_count, LEFT), jnp.float32),
            pltpu.VMEM((LEAD + q_count, RIGHT), jnp.float32),
            dma((2,)),
            dma((2 * across,)),
            dma((2 * across,)),
            dma((2,)),
            dma((2 * pair * chunks,)),
            dma((2 * pair * chunks,)),
            dma((2,)),
            dma((2,)),
        ],
        compiler_params=pltpu.CompilerParams(
            collective_id=0, has_side_effects=True, vmem_limit_bytes=48 << 20
        ),
        name="scores",
    )(queries, map_descriptors)


def best_kernel(slopes_ref, ext_ref, out_ref, c_ref, a2_ref, a4_ref, a8_ref):
    pb, ma = lax.axis_index("pb"), lax.axis_index("ma")
    rows, width = ext_ref.shape
    q_count, m_count = rows - LEAD, width - LEFT - RIGHT
    halo = LEFT // LANES
    tiles = halo + m_count // LANES
    size = 2 * RAD + 1

    def window(value):
        two = value + pltpu.roll(value, 1, 1)
        four = two + pltpu.roll(two, 2, 1)
        eight = four + pltpu.roll(four, 4, 1)
        sixteen = eight + pltpu.roll(eight, 8, 1)
        total = sixteen + pltpu.roll(four, 16, 1) + pltpu.roll(value, 20, 1)
        return pltpu.roll(total, width - RAD, 1) * (1.0 / size)

    group = 16
    first_row = jnp.where(pb == 0, LEAD, 0)
    first_col = jnp.where(ma == 0, LEFT, 0)

    @pl.loop(0, rows // group)
    def _(number):
        at = pl.multiple_of(number * group, group)
        value = ext_ref[pl.ds(at, group), :]
        average = window(value)
        spread = window(value * value) - average * average
        normal = (value - average) * (lax.rsqrt(spread + 1.0) * (1.0 / math.sqrt(SEQ)))
        row = lax.broadcasted_iota(jnp.int32, (group, width), 0) + at
        col = lax.broadcasted_iota(jnp.int32, (group, width), 1)
        normal = jnp.where((row >= first_row) & (col >= first_col), normal, 0.0)
        for tile in range(tiles):
            c_ref[tile, pl.ds(at, group), :] = normal[:, tile * LANES : (tile + 1) * LANES]

    out_ref[0] = jnp.full((q_count, m_count), -jnp.inf, jnp.float32)

    def moved(ref, tile, at, count, shift, lane, before):
        here = pltpu.roll(ref[tile, pl.ds(at, count), :], shift, 1)
        return here, jnp.where(lane < shift, here if before is None else before, here)

    def add(dst, src, lag, shift, start, count, low):
        lane = lax.broadcasted_iota(jnp.int32, (count, LANES), 1)

        @pl.loop(0, (rows - start) // count)
        def _(number):
            at = pl.multiple_of(start + number * count, 8)
            before = None
            if low > 0:
                before = pltpu.roll(src[low - 1, pl.ds(at - lag, count), :], shift, 1)
            for tile in range(low, tiles):
                before, other = moved(src, tile, at - lag, count, shift, lane, before)
                dst[tile, pl.ds(at, count), :] = src[tile, pl.ds(at, count), :] + other

    @pl.loop(0, slopes_ref.shape[0])
    def _(index):
        v = slopes_ref[index]
        add(a2_ref, c_ref, 1, v, 8, 40, 0)
        add(a4_ref, a2_ref, 2, 2 * v, 16, 16, halo - 2)
        add(a8_ref, a4_ref, 4, 4 * v, 24, 24, halo - 1)
        far = 16 * v
        back, rest = far // LANES, far % LANES
        count = 32
        lane = lax.broadcasted_iota(jnp.int32, (count, LANES), 1)

        @pl.loop(0, q_count // count)
        def _(number):
            at = pl.multiple_of(LEAD + number * count, 8)
            low = halo - 1
            before8 = pltpu.roll(a8_ref[low, pl.ds(at - 8, count), :], 8 * v, 1)
            before4 = pltpu.roll(a4_ref[low - back, pl.ds(at - 16, count), :], rest, 1)
            for tile in range(halo, tiles):
                before8, eight = moved(a8_ref, tile, at - 8, count, 8 * v, lane, before8)
                before4, four = moved(a4_ref, tile - back, at - 16, count, rest, lane, before4)
                total = a8_ref[tile, pl.ds(at, count), :] + eight + four
                to = pl.multiple_of(number * count, 8)
                cols = pl.ds((tile - halo) * LANES, LANES)
                out_ref[0, pl.ds(to, count), cols] = jnp.maximum(
                    out_ref[0, pl.ds(to, count), cols], total
                )


def sequence_best(extended, slopes):
    rows, width = extended.shape
    m_count = width - LEFT - RIGHT
    tiles = (LEFT + m_count) // LANES
    return pl.pallas_call(
        best_kernel,
        out_shape=jax.ShapeDtypeStruct((1, rows - LEAD, m_count), jnp.float32),
        in_specs=[
            pl.BlockSpec(memory_space=pltpu.SMEM),
            pl.BlockSpec(memory_space=pltpu.VMEM),
        ],
        out_specs=pl.BlockSpec(memory_space=pltpu.VMEM),
        scratch_shapes=[pltpu.VMEM((tiles, rows, LANES), jnp.float32)] * 4,
        compiler_params=pltpu.CompilerParams(vmem_limit_bytes=32 << 20),
        name="best",
    )(slopes, extended)


def solution(mesh):
    npb, nma = mesh.shape["pb"], mesh.shape["ma"]

    def local(queries, map_descriptors, slopes):
        return sequence_best(score_tile(queries, map_descriptors, npb, nma), slopes)

    return jax.shard_map(
        local,
        mesh=mesh,
        in_specs=(P(None, ("pb", "ma"), None), P("ma", "pb"), P()),
        out_specs=P(None, "pb", "ma"),
        check_vma=False,
    )
```

```python
import math

import jax
import jax.numpy as jnp
from jax import lax
from jax.experimental import pallas as pl
from jax.experimental.pallas import tpu as pltpu
from jax.sharding import PartitionSpec as P

MESH = pl.DeviceIdType.MESH
SEQ = 20
RAD = 10
LEAD = 32
LEFT = 384
RIGHT = 128
LANES = 128
CORES = 2


def remote(src, dst, send, recv, where):
    return pltpu.make_async_remote_copy(
        src_ref=src,
        dst_ref=dst,
        send_sem=send,
        recv_sem=recv,
        device_id=where,
        device_id_type=MESH,
    )


def score_kernel(
    npb,
    nma,
    chunks,
    q_ref,
    m_ref,
    out_ref,
    q_all,
    q_lead,
    m_all,
    scores,
    left,
    right,
    local_sem,
    q_send,
    q_recv,
    lead_sem,
    m_send,
    m_recv,
    halo_send,
    halo_recv,
):
    pb, ma = lax.axis_index("pb"), lax.axis_index("ma")
    pair, across = npb // CORES, nma // 2
    row, core = pb // CORES, pb % CORES
    z, x = ma // 2, ma % 2
    mate = row * CORES + 1 - core
    twin = z * 2 + 1 - x
    rows_other = [((row + i) % pair) * CORES + core for i in range(1, pair)]
    rows_from = [((row + pair - i) % pair) * CORES + core for i in range(1, pair)]
    z_other = [((z + i) % across) * 2 + x for i in range(1, across)]
    z_from = [((z + across - i) % across) * 2 + x for i in range(1, across)]
    has_up, has_down = pb > 0, pb < npb - 1
    has_left, has_right = ma > 0, ma < nma - 1

    load_q = pltpu.make_async_copy(q_ref.at[0], q_all.at[ma], local_sem.at[0])
    load_q.start()
    load_m = pltpu.make_async_copy(m_ref, m_all.at[pb], local_sem.at[1])
    load_m.start()

    barrier = pltpu.get_barrier_semaphore()

    def greet(where):
        pl.semaphore_signal(barrier, inc=1, device_id=where, device_id_type=MESH)

    greet({"pb": mate})
    greet({"ma": twin})
    for other in rows_other:
        greet({"pb": other})
    for other in z_other:
        greet({"ma": other})
    for test, where in (
        (has_up, {"pb": pb - 1}),
        (has_down, {"pb": pb + 1}),
        (has_left, {"ma": ma - 1}),
        (has_right, {"ma": ma + 1}),
    ):

        @pl.when(test)
        def _():
            greet(where)

    edges = sum(
        jnp.where(test, 1, 0) for test in (has_up, has_down, has_left, has_right)
    )
    pl.semaphore_wait(barrier, pair + across + edges)

    load_q.wait()
    q_to_z = [
        remote(q_all.at[ma], q_all.at[ma], q_send.at[i], q_recv.at[i], {"ma": other})
        for i, other in enumerate(z_other)
    ]
    for copy in q_to_z:
        copy.start()
    first = across - 1
    q_to_x = [
        remote(
            q_all.at[ma], q_all.at[ma], q_send.at[first], q_recv.at[first], {"ma": twin}
        )
    ]
    q_to_x[0].start()

    load_m.wait()
    m_count = m_ref.shape[0]
    step = m_count // chunks
    order = list(range(chunks - 1, chunks // 2 - 1, -1)) + list(range(chunks // 2))

    def piece(slot, chunk):
        return m_all.at[slot, pl.ds(chunk * step, step)]

    m_to_row, m_to_mate = {}, {}
    for chunk in order:
        for i, other in enumerate(rows_other):
            at = i * chunks + chunk
            m_to_row[i, chunk] = remote(
                piece(pb, chunk), piece(pb, chunk), m_send.at[at], m_recv.at[at], {"pb": other}
            )
            m_to_row[i, chunk].start()
    for chunk in order:
        at = (pair - 1) * chunks + chunk
        m_to_mate[-1, chunk] = remote(
            piece(pb, chunk), piece(pb, chunk), m_send.at[at], m_recv.at[at], {"pb": mate}
        )
        m_to_mate[-1, chunk].start()

    for i, source in enumerate(z_from):
        q_to_z[i].wait_recv()
        at = across + i
        copy = remote(
            q_all.at[source], q_all.at[source], q_send.at[at], q_recv.at[at], {"ma": twin}
        )
        copy.start()
        q_to_x.append(copy)
    for copy in q_to_x:
        copy.wait_recv()

    held = q_lead.shape[0]
    lead = remote(
        q_all.at[pl.ds(nma - held, held)], q_lead, lead_sem.at[0], lead_sem.at[1], {"pb": pb + 1}
    )

    @pl.when(has_down)
    def _():
        lead.start()

    @pl.when(pb == 0)
    def _():
        q_lead[...] = jnp.zeros_like(q_lead)

    @pl.when(ma == 0)
    def _():
        left[...] = jnp.zeros_like(left)

    @pl.when(ma == nma - 1)
    def _():
        right[...] = jnp.zeros_like(right)

    def flat(ref):
        count, each, width = ref.shape
        if each % 16 == 0:
            return ref[...].reshape(count * each, width)
        return ref[...].astype(jnp.float32).reshape(count * each, width).astype(ref.dtype)

    to_right = remote(
        scores.at[:, pl.ds(m_count - LEFT, LEFT)],
        left,
        halo_send.at[0],
        halo_recv.at[0],
        {"ma": ma + 1},
    )
    to_left = remote(
        scores.at[:, pl.ds(0, RIGHT)],
        right,
        halo_send.at[1],
        halo_recv.at[1],
        {"ma": ma - 1},
    )
    done = set()
    for number, chunk in enumerate(order):
        for i, source in enumerate(rows_from):
            m_to_row[i, chunk].wait_recv()
            at = (pair + i) * chunks + chunk
            m_to_mate[i, chunk] = remote(
                piece(source, chunk), piece(source, chunk), m_send.at[at], m_recv.at[at], {"pb": mate}
            )
            m_to_mate[i, chunk].start()
        for i in range(-1, pair - 1):
            m_to_mate[i, chunk].wait_recv()
        if number == 0:

            @pl.when(has_up)
            def _():
                lead.wait_recv()

        k = m_ref.shape[1]
        for queries, at in ((q_lead, 0), (q_all, LEAD)):
            total = None
            block = flat(queries)
            for slot in range(npb):
                part = lax.dot_general(
                    block[:, slot * k : (slot + 1) * k],
                    m_all[slot, pl.ds(chunk * step, step), :],
                    (((1,), (1,)), ((), ())),
                    preferred_element_type=jnp.float32,
                )
                total = part if total is None else total + part
            scores[pl.ds(at, block.shape[0]), pl.ds(chunk * step, step)] = total
        before = set(done)
        done.update(range(chunk * step, (chunk + 1) * step, LANES))
        right_part = set(range(m_count - LEFT, m_count, LANES))
        left_part = set(range(0, RIGHT, LANES))
        if right_part <= done and not right_part <= before:

            @pl.when(has_right)
            def _():
                to_right.start()

        if left_part <= done and not left_part <= before:

            @pl.when(has_left)
            def _():
                to_left.start()

    out_ref[:, pl.ds(LEFT, m_count)] = scores[...]

    @pl.when(has_left)
    def _():
        to_right.wait_recv()

    out_ref[:, pl.ds(0, LEFT)] = left[...]

    @pl.when(has_right)
    def _():
        to_left.wait_recv()

    out_ref[:, pl.ds(LEFT + m_count, RIGHT)] = right[...]

    for copy in q_to_z + q_to_x + list(m_to_row.values()) + list(m_to_mate.values()):
        copy.wait_send()

    @pl.when(has_down)
    def _():
        lead.wait_send()

    @pl.when(has_right)
    def _():
        to_right.wait_send()

    @pl.when(has_left)
    def _():
        to_left.wait_send()


def score_tile(queries, map_descriptors, npb, nma):
    each, width = queries.shape[1:]
    m_count, k = map_descriptors.shape
    q_count = each * nma
    chunks = 4
    held = LEAD // each
    pair, across = npb // CORES, nma // 2
    dma = pltpu.SemaphoreType.DMA
    return pl.pallas_call(
        lambda *refs: score_kernel(npb, nma, chunks, *refs),
        out_shape=jax.ShapeDtypeStruct(
            (LEAD + q_count, LEFT + m_count + RIGHT), jnp.float32
        ),
        in_specs=[pl.BlockSpec(memory_space=pl.ANY)] * 2,
        out_specs=pl.BlockSpec(memory_space=pltpu.VMEM),
        scratch_shapes=[
            pltpu.VMEM((nma, each, width), jnp.bfloat16),
            pltpu.VMEM((held, each, width), jnp.bfloat16),
            pltpu.VMEM((npb, m_count, k), jnp.bfloat16),
            pltpu.VMEM((LEAD + q_count, m_count), jnp.float32),
            pltpu.VMEM((LEAD + q_count, LEFT), jnp.float32),
            pltpu.VMEM((LEAD + q_count, RIGHT), jnp.float32),
            dma((2,)),
            dma((2 * across,)),
            dma((2 * across,)),
            dma((2,)),
            dma((2 * pair * chunks,)),
            dma((2 * pair * chunks,)),
            dma((2,)),
            dma((2,)),
        ],
        compiler_params=pltpu.CompilerParams(
            collective_id=0, has_side_effects=True, vmem_limit_bytes=48 << 20
        ),
        name="scores",
    )(queries, map_descriptors)


def best_kernel(slopes_ref, ext_ref, out_ref, c_ref, a2_ref, a4_ref, a8_ref):
    pb, ma = lax.axis_index("pb"), lax.axis_index("ma")
    rows, width = ext_ref.shape
    q_count, m_count = rows - LEAD, width - LEFT - RIGHT
    halo = LEFT // LANES
    tiles = halo + m_count // LANES
    size = 2 * RAD + 1

    def window(value):
        two = value + pltpu.roll(value, 1, 1)
        four = two + pltpu.roll(two, 2, 1)
        eight = four + pltpu.roll(four, 4, 1)
        sixteen = eight + pltpu.roll(eight, 8, 1)
        total = sixteen + pltpu.roll(four, 16, 1) + pltpu.roll(value, 20, 1)
        return pltpu.roll(total, width - RAD, 1) * (1.0 / size)

    group = 16
    first_row = jnp.where(pb == 0, LEAD, 0)
    first_col = jnp.where(ma == 0, LEFT, 0)

    @pl.loop(0, rows // group)
    def _(number):
        at = pl.multiple_of(number * group, group)
        value = ext_ref[pl.ds(at, group), :]
        average = window(value)
        spread = window(value * value) - average * average
        normal = (value - average) * (lax.rsqrt(spread + 1.0) * (1.0 / math.sqrt(SEQ)))
        row = lax.broadcasted_iota(jnp.int32, (group, width), 0) + at
        col = lax.broadcasted_iota(jnp.int32, (group, width), 1)
        normal = jnp.where((row >= first_row) & (col >= first_col), normal, 0.0)
        for tile in range(tiles):
            c_ref[tile, pl.ds(at, group), :] = normal[:, tile * LANES : (tile + 1) * LANES]

    out_ref[0] = jnp.full((q_count, m_count), -jnp.inf, jnp.float32)

    def moved(ref, tile, at, count, shift, lane, before):
        here = pltpu.roll(ref[tile, pl.ds(at, count), :], shift, 1)
        return here, jnp.where(lane < shift, here if before is None else before, here)

    def add(dst, src, lag, shift, base, start, count, low):
        lane = lax.broadcasted_iota(jnp.int32, (count, LANES), 1)
        for first in range(start, rows, count):
            at = base + first
            before = None
            if low > 0:
                before = pltpu.roll(src[low - 1, pl.ds(at - lag, count), :], shift, 1)
            for tile in range(low, tiles):
                before, other = moved(src, tile, at - lag, count, shift, lane, before)
                dst[tile, pl.ds(at, count), :] = src[tile, pl.ds(at, count), :] + other

    @pl.loop(0, slopes_ref.shape[0])
    def _(index):
        v = slopes_ref[index]
        base = pl.multiple_of((v // 16) * 8, 8)
        add(a2_ref, c_ref, 1, v, base, 8, 40, 0)
        add(a4_ref, a2_ref, 2, 2 * v, base, 16, 16, halo - 2)
        add(a8_ref, a4_ref, 4, 4 * v, base, 24, 24, halo - 1)
        far = 16 * v
        back, rest = far // LANES, far % LANES
        count = 16
        lane = lax.broadcasted_iota(jnp.int32, (count, LANES), 1)
        for first in range(0, q_count, count):
            at = base + (LEAD + first)
            low = halo - 1
            before8 = pltpu.roll(a8_ref[low, pl.ds(at - 8, count), :], 8 * v, 1)
            before4 = pltpu.roll(a4_ref[low - back, pl.ds(at - 16, count), :], rest, 1)
            for tile in range(halo, tiles):
                before8, eight = moved(a8_ref, tile, at - 8, count, 8 * v, lane, before8)
                before4, four = moved(a4_ref, tile - back, at - 16, count, rest, lane, before4)
                total = a8_ref[tile, pl.ds(at, count), :] + eight + four
                cols = pl.ds((tile - halo) * LANES, LANES)
                out_ref[0, pl.ds(first, count), cols] = jnp.maximum(
                    out_ref[0, pl.ds(first, count), cols], total
                )


def sequence_best(extended, slopes):
    rows, width = extended.shape
    m_count = width - LEFT - RIGHT
    tiles = (LEFT + m_count) // LANES
    return pl.pallas_call(
        best_kernel,
        out_shape=jax.ShapeDtypeStruct((1, rows - LEAD, m_count), jnp.float32),
        in_specs=[
            pl.BlockSpec(memory_space=pltpu.SMEM),
            pl.BlockSpec(memory_space=pltpu.VMEM),
        ],
        out_specs=pl.BlockSpec(memory_space=pltpu.VMEM),
        scratch_shapes=[pltpu.VMEM((tiles, rows, LANES), jnp.float32)] * 4,
        compiler_params=pltpu.CompilerParams(vmem_limit_bytes=32 << 20),
        name="best",
    )(slopes, extended)


def solution(mesh):
    npb, nma = mesh.shape["pb"], mesh.shape["ma"]

    def local(queries, map_descriptors, slopes):
        return sequence_best(score_tile(queries, map_descriptors, npb, nma), slopes)

    return jax.shard_map(
        local,
        mesh=mesh,
        in_specs=(P(None, ("pb", "ma"), None), P("ma", "pb"), P()),
        out_specs=P(None, "pb", "ma"),
        check_vma=False,
    )
```

```python
import math

import jax
import jax.numpy as jnp
from jax import lax
from jax.experimental import pallas as pl
from jax.experimental.pallas import tpu as pltpu
from jax.sharding import PartitionSpec as P

MESH = pl.DeviceIdType.MESH
SEQ = 20
RAD = 10
LEAD = 32
LEFT = 384
RIGHT = 128
LANES = 128
CORES = 2


def remote(src, dst, send, recv, where):
    return pltpu.make_async_remote_copy(
        src_ref=src,
        dst_ref=dst,
        send_sem=send,
        recv_sem=recv,
        device_id=where,
        device_id_type=MESH,
    )


def score_kernel(
    npb,
    nma,
    chunks,
    q_ref,
    m_ref,
    out_ref,
    q_all,
    q_lead,
    m_all,
    scores,
    left,
    right,
    local_sem,
    q_send,
    q_recv,
    lead_sem,
    m_send,
    m_recv,
    halo_send,
    halo_recv,
):
    pb, ma = lax.axis_index("pb"), lax.axis_index("ma")
    pair, across = npb // CORES, nma // 2
    row, core = pb // CORES, pb % CORES
    z, x = ma // 2, ma % 2
    mate = row * CORES + 1 - core
    twin = z * 2 + 1 - x
    rows_other = [((row + i) % pair) * CORES + core for i in range(1, pair)]
    rows_from = [((row + pair - i) % pair) * CORES + core for i in range(1, pair)]
    z_other = [((z + i) % across) * 2 + x for i in range(1, across)]
    z_from = [((z + across - i) % across) * 2 + x for i in range(1, across)]
    has_up, has_down = pb > 0, pb < npb - 1
    has_left, has_right = ma > 0, ma < nma - 1

    load_q = pltpu.make_async_copy(q_ref.at[0], q_all.at[ma], local_sem.at[0])
    load_q.start()
    load_m = pltpu.make_async_copy(m_ref, m_all.at[pb], local_sem.at[1])
    load_m.start()

    barrier = pltpu.get_barrier_semaphore()

    def greet(where):
        pl.semaphore_signal(barrier, inc=1, device_id=where, device_id_type=MESH)

    greet({"pb": mate})
    greet({"ma": twin})
    for other in rows_other:
        greet({"pb": other})
    for other in z_other:
        greet({"ma": other})
    for test, where in (
        (has_up, {"pb": pb - 1}),
        (has_down, {"pb": pb + 1}),
        (has_left, {"ma": ma - 1}),
        (has_right, {"ma": ma + 1}),
    ):

        @pl.when(test)
        def _():
            greet(where)

    edges = sum(
        jnp.where(test, 1, 0) for test in (has_up, has_down, has_left, has_right)
    )
    pl.semaphore_wait(barrier, pair + across + edges)

    load_q.wait()
    q_to_z = [
        remote(q_all.at[ma], q_all.at[ma], q_send.at[i], q_recv.at[i], {"ma": other})
        for i, other in enumerate(z_other)
    ]
    for copy in q_to_z:
        copy.start()
    first = across - 1
    q_to_x = [
        remote(
            q_all.at[ma], q_all.at[ma], q_send.at[first], q_recv.at[first], {"ma": twin}
        )
    ]
    q_to_x[0].start()

    load_m.wait()
    m_count = m_ref.shape[0]
    step = m_count // chunks
    order = list(range(chunks - 1, chunks // 2 - 1, -1)) + list(range(chunks // 2))

    def piece(slot, chunk):
        return m_all.at[slot, pl.ds(chunk * step, step)]

    m_to_row, m_to_mate = {}, {}
    for chunk in order:
        for i, other in enumerate(rows_other):
            at = i * chunks + chunk
            m_to_row[i, chunk] = remote(
                piece(pb, chunk), piece(pb, chunk), m_send.at[at], m_recv.at[at], {"pb": other}
            )
            m_to_row[i, chunk].start()
    for chunk in order:
        at = (pair - 1) * chunks + chunk
        m_to_mate[-1, chunk] = remote(
            piece(pb, chunk), piece(pb, chunk), m_send.at[at], m_recv.at[at], {"pb": mate}
        )
        m_to_mate[-1, chunk].start()

    for i, source in enumerate(z_from):
        q_to_z[i].wait_recv()
        at = across + i
        copy = remote(
            q_all.at[source], q_all.at[source], q_send.at[at], q_recv.at[at], {"ma": twin}
        )
        copy.start()
        q_to_x.append(copy)
    for copy in q_to_x:
        copy.wait_recv()

    held = q_lead.shape[0]
    lead = remote(
        q_all.at[pl.ds(nma - held, held)], q_lead, lead_sem.at[0], lead_sem.at[1], {"pb": pb + 1}
    )

    @pl.when(has_down)
    def _():
        lead.start()

    @pl.when(pb == 0)
    def _():
        q_lead[...] = jnp.zeros_like(q_lead)

    @pl.when(ma == 0)
    def _():
        left[...] = jnp.zeros_like(left)

    @pl.when(ma == nma - 1)
    def _():
        right[...] = jnp.zeros_like(right)

    def flat(ref):
        count, each, width = ref.shape
        if each % 16 == 0:
            return ref[...].reshape(count * each, width)
        return ref[...].astype(jnp.float32).reshape(count * each, width).astype(ref.dtype)

    to_right = remote(
        scores.at[:, pl.ds(m_count - LEFT, LEFT)],
        left,
        halo_send.at[0],
        halo_recv.at[0],
        {"ma": ma + 1},
    )
    to_left = remote(
        scores.at[:, pl.ds(0, RIGHT)],
        right,
        halo_send.at[1],
        halo_recv.at[1],
        {"ma": ma - 1},
    )
    done = set()
    for number, chunk in enumerate(order):
        for i, source in enumerate(rows_from):
            m_to_row[i, chunk].wait_recv()
            at = (pair + i) * chunks + chunk
            m_to_mate[i, chunk] = remote(
                piece(source, chunk), piece(source, chunk), m_send.at[at], m_recv.at[at], {"pb": mate}
            )
            m_to_mate[i, chunk].start()
        for i in range(-1, pair - 1):
            m_to_mate[i, chunk].wait_recv()
        if number == 0:

            @pl.when(has_up)
            def _():
                lead.wait_recv()

        k = m_ref.shape[1]
        for queries, at in ((q_lead, 0), (q_all, LEAD)):
            total = None
            block = flat(queries)
            for slot in range(npb):
                part = lax.dot_general(
                    block[:, slot * k : (slot + 1) * k],
                    m_all[slot, pl.ds(chunk * step, step), :],
                    (((1,), (1,)), ((), ())),
                    preferred_element_type=jnp.float32,
                )
                total = part if total is None else total + part
            scores[pl.ds(at, block.shape[0]), pl.ds(chunk * step, step)] = total
        before = set(done)
        done.update(range(chunk * step, (chunk + 1) * step, LANES))
        right_part = set(range(m_count - LEFT, m_count, LANES))
        left_part = set(range(0, RIGHT, LANES))
        if right_part <= done and not right_part <= before:

            @pl.when(has_right)
            def _():
                to_right.start()

        if left_part <= done and not left_part <= before:

            @pl.when(has_left)
            def _():
                to_left.start()

    out_ref[:, pl.ds(LEFT, m_count)] = scores[...]

    @pl.when(has_left)
    def _():
        to_right.wait_recv()

    out_ref[:, pl.ds(0, LEFT)] = left[...]

    @pl.when(has_right)
    def _():
        to_left.wait_recv()

    out_ref[:, pl.ds(LEFT + m_count, RIGHT)] = right[...]

    for copy in q_to_z + q_to_x + list(m_to_row.values()) + list(m_to_mate.values()):
        copy.wait_send()

    @pl.when(has_down)
    def _():
        lead.wait_send()

    @pl.when(has_right)
    def _():
        to_right.wait_send()

    @pl.when(has_left)
    def _():
        to_left.wait_send()


def score_tile(queries, map_descriptors, npb, nma):
    each, width = queries.shape[1:]
    m_count, k = map_descriptors.shape
    q_count = each * nma
    chunks = 4
    held = LEAD // each
    pair, across = npb // CORES, nma // 2
    dma = pltpu.SemaphoreType.DMA
    return pl.pallas_call(
        lambda *refs: score_kernel(npb, nma, chunks, *refs),
        out_shape=jax.ShapeDtypeStruct(
            (LEAD + q_count, LEFT + m_count + RIGHT), jnp.float32
        ),
        in_specs=[pl.BlockSpec(memory_space=pl.ANY)] * 2,
        out_specs=pl.BlockSpec(memory_space=pltpu.VMEM),
        scratch_shapes=[
            pltpu.VMEM((nma, each, width), jnp.bfloat16),
            pltpu.VMEM((held, each, width), jnp.bfloat16),
            pltpu.VMEM((npb, m_count, k), jnp.bfloat16),
            pltpu.VMEM((LEAD + q_count, m_count), jnp.float32),
            pltpu.VMEM((LEAD + q_count, LEFT), jnp.float32),
            pltpu.VMEM((LEAD + q_count, RIGHT), jnp.float32),
            dma((2,)),
            dma((2 * across,)),
            dma((2 * across,)),
            dma((2,)),
            dma((2 * pair * chunks,)),
            dma((2 * pair * chunks,)),
            dma((2,)),
            dma((2,)),
        ],
        compiler_params=pltpu.CompilerParams(
            collective_id=0, has_side_effects=True, vmem_limit_bytes=48 << 20
        ),
        name="scores",
    )(queries, map_descriptors)


def best_kernel(slopes_ref, ext_ref, out_ref, c_ref, a2_ref, a4_ref, a8_ref):
    pb, ma = lax.axis_index("pb"), lax.axis_index("ma")
    rows, width = ext_ref.shape
    q_count, m_count = rows - LEAD, width - LEFT - RIGHT
    halo = LEFT // LANES
    tiles = halo + m_count // LANES
    size = 2 * RAD + 1

    block = 2 * LANES

    def band_of(depth, width, lead):
        inner = lax.broadcasted_iota(jnp.int32, (depth, width), 0)
        outer = lax.broadcasted_iota(jnp.int32, (depth, width), 1)
        near = jnp.abs(inner - lead - outer) <= RAD
        return jnp.where(near, 1.0, 0.0).astype(jnp.bfloat16)

    def window(value, band):
        total = None
        for _ in range(3):
            part = value.astype(jnp.bfloat16)
            value = value - part.astype(jnp.float32)
            term = jnp.dot(part, band, preferred_element_type=jnp.float32)
            total = term if total is None else total + term
        return total * (1.0 / size)

    group = 96
    first_row = jnp.where(pb == 0, LEAD, 0)
    first_col = jnp.where(ma == 0, LEFT, 0)
    edge = band_of(block, LANES, 0)
    inside = band_of(2 * block, block, LANES)

    def contrast(at, tile, lead, count, band):
        begin = tile * LANES - lead
        value = ext_ref[pl.ds(at, group), pl.ds(begin, band.shape[0])]
        centre = value[:, lead : lead + count * LANES]
        average = window(value, band)
        spread = window(value * value, band) - average * average
        normal = (centre - average) * (
            lax.rsqrt(spread + 1.0) * (1.0 / math.sqrt(SEQ))
        )
        row = lax.broadcasted_iota(jnp.int32, normal.shape, 0) + at
        col = lax.broadcasted_iota(jnp.int32, normal.shape, 1) + tile * LANES
        seen = (row >= first_row) & (col >= first_col)
        normal = jnp.where(seen, normal, 0.0)
        for half in range(count):
            c_ref[tile + half, pl.ds(at, group), :] = normal[
                :, half * LANES : (half + 1) * LANES
            ]

    @pl.loop(0, rows // group)
    def _(number):
        at = pl.multiple_of(number * group, 8)
        contrast(at, 0, 0, 1, edge)
        for tile in range(1, tiles, 2):
            contrast(at, tile, LANES, 2, inside)

    out_ref[0] = jnp.full((q_count, m_count), -jnp.inf, jnp.float32)

    def moved(ref, tile, at, count, shift, lane, before):
        here = pltpu.roll(ref[tile, pl.ds(at, count), :], shift, 1)
        return here, jnp.where(lane < shift, here if before is None else before, here)

    def add(dst, src, lag, shift, base, start, count, low):
        lane = lax.broadcasted_iota(jnp.int32, (count, LANES), 1)
        for first in range(start, rows, count):
            at = base + first
            before = None
            if low > 0:
                before = pltpu.roll(src[low - 1, pl.ds(at - lag, count), :], shift, 1)
            for tile in range(low, tiles):
                before, other = moved(src, tile, at - lag, count, shift, lane, before)
                dst[tile, pl.ds(at, count), :] = src[tile, pl.ds(at, count), :] + other

    @pl.loop(0, slopes_ref.shape[0])
    def _(index):
        v = slopes_ref[index]
        base = pl.multiple_of((v // 16) * 8, 8)
        add(a2_ref, c_ref, 1, v, base, 8, 40, 0)
        add(a4_ref, a2_ref, 2, 2 * v, base, 16, 16, halo - 2)
        add(a8_ref, a4_ref, 4, 4 * v, base, 24, 24, halo - 1)
        far = 16 * v
        back, rest = far // LANES, far % LANES
        count = 16
        lane = lax.broadcasted_iota(jnp.int32, (count, LANES), 1)
        for first in range(0, q_count, count):
            at = base + (LEAD + first)
            low = halo - 1
            before8 = pltpu.roll(a8_ref[low, pl.ds(at - 8, count), :], 8 * v, 1)
            before4 = pltpu.roll(a4_ref[low - back, pl.ds(at - 16, count), :], rest, 1)
            for tile in range(halo, tiles):
                before8, eight = moved(a8_ref, tile, at - 8, count, 8 * v, lane, before8)
                before4, four = moved(a4_ref, tile - back, at - 16, count, rest, lane, before4)
                total = a8_ref[tile, pl.ds(at, count), :] + eight + four
                cols = pl.ds((tile - halo) * LANES, LANES)
                out_ref[0, pl.ds(first, count), cols] = jnp.maximum(
                    out_ref[0, pl.ds(first, count), cols], total
                )


def sequence_best(extended, slopes):
    rows, width = extended.shape
    m_count = width - LEFT - RIGHT
    tiles = (LEFT + m_count) // LANES
    return pl.pallas_call(
        best_kernel,
        out_shape=jax.ShapeDtypeStruct((1, rows - LEAD, m_count), jnp.float32),
        in_specs=[
            pl.BlockSpec(memory_space=pltpu.SMEM),
            pl.BlockSpec(memory_space=pltpu.VMEM),
        ],
        out_specs=pl.BlockSpec(memory_space=pltpu.VMEM),
        scratch_shapes=[pltpu.VMEM((tiles, rows, LANES), jnp.float32)] * 4,
        compiler_params=pltpu.CompilerParams(vmem_limit_bytes=32 << 20),
        name="best",
    )(slopes, extended)


def solution(mesh):
    npb, nma = mesh.shape["pb"], mesh.shape["ma"]

    def local(queries, map_descriptors, slopes):
        return sequence_best(score_tile(queries, map_descriptors, npb, nma), slopes)

    return jax.shard_map(
        local,
        mesh=mesh,
        in_specs=(P(None, ("pb", "ma"), None), P("ma", "pb"), P()),
        out_specs=P(None, "pb", "ma"),
        check_vma=False,
    )
```

```python
import math

import jax
import jax.numpy as jnp
from jax import lax
from jax.experimental import pallas as pl
from jax.experimental.pallas import tpu as pltpu
from jax.sharding import PartitionSpec as P

MESH = pl.DeviceIdType.MESH
SEQ = 20
RAD = 10
LEAD = 32
LEFT = 384
RIGHT = 128
LANES = 128
CORES = 2


def remote(src, dst, send, recv, where):
    return pltpu.make_async_remote_copy(
        src_ref=src,
        dst_ref=dst,
        send_sem=send,
        recv_sem=recv,
        device_id=where,
        device_id_type=MESH,
    )


def score_kernel(
    npb,
    nma,
    chunks,
    q_ref,
    m_ref,
    out_ref,
    q_all,
    q_lead,
    m_all,
    scores,
    left,
    right,
    local_sem,
    q_send,
    q_recv,
    lead_sem,
    m_send,
    m_recv,
    halo_send,
    halo_recv,
):
    pb, ma = lax.axis_index("pb"), lax.axis_index("ma")
    pair, across = npb // CORES, nma // 2
    row, core = pb // CORES, pb % CORES
    z, x = ma // 2, ma % 2
    mate = row * CORES + 1 - core
    twin = z * 2 + 1 - x
    rows_other = [((row + i) % pair) * CORES + core for i in range(1, pair)]
    rows_from = [((row + pair - i) % pair) * CORES + core for i in range(1, pair)]
    z_other = [((z + i) % across) * 2 + x for i in range(1, across)]
    z_from = [((z + across - i) % across) * 2 + x for i in range(1, across)]
    has_up, has_down = pb > 0, pb < npb - 1
    has_left, has_right = ma > 0, ma < nma - 1

    load_q = pltpu.make_async_copy(q_ref.at[0], q_all.at[ma], local_sem.at[0])
    load_q.start()
    load_m = pltpu.make_async_copy(m_ref, m_all.at[pb], local_sem.at[1])
    load_m.start()

    barrier = pltpu.get_barrier_semaphore()

    def greet(where):
        pl.semaphore_signal(barrier, inc=1, device_id=where, device_id_type=MESH)

    greet({"pb": mate})
    greet({"ma": twin})
    for other in rows_other:
        greet({"pb": other})
    for other in z_other:
        greet({"ma": other})
    for test, where in (
        (has_up, {"pb": pb - 1}),
        (has_down, {"pb": pb + 1}),
        (has_left, {"ma": ma - 1}),
        (has_right, {"ma": ma + 1}),
    ):

        @pl.when(test)
        def _():
            greet(where)

    edges = sum(
        jnp.where(test, 1, 0) for test in (has_up, has_down, has_left, has_right)
    )
    pl.semaphore_wait(barrier, pair + across + edges)

    load_q.wait()
    q_to_z = [
        remote(q_all.at[ma], q_all.at[ma], q_send.at[i], q_recv.at[i], {"ma": other})
        for i, other in enumerate(z_other)
    ]
    for copy in q_to_z:
        copy.start()
    first = across - 1
    q_to_x = [
        remote(
            q_all.at[ma], q_all.at[ma], q_send.at[first], q_recv.at[first], {"ma": twin}
        )
    ]
    q_to_x[0].start()

    load_m.wait()
    m_count = m_ref.shape[0]
    step = m_count // chunks
    order = list(range(chunks - 1, chunks // 2 - 1, -1)) + list(range(chunks // 2))

    def piece(slot, chunk):
        return m_all.at[slot, pl.ds(chunk * step, step)]

    m_to_row, m_to_mate = {}, {}
    for chunk in order:
        for i, other in enumerate(rows_other):
            at = i * chunks + chunk
            m_to_row[i, chunk] = remote(
                piece(pb, chunk), piece(pb, chunk), m_send.at[at], m_recv.at[at], {"pb": other}
            )
            if chunk != order[-1]:
                m_to_row[i, chunk].start()
    for chunk in order:
        at = (pair - 1) * chunks + chunk
        m_to_mate[-1, chunk] = remote(
            piece(pb, chunk), piece(pb, chunk), m_send.at[at], m_recv.at[at], {"pb": mate}
        )
        m_to_mate[-1, chunk].start()

    for i, source in enumerate(z_from):
        q_to_z[i].wait_recv()
        at = across + i
        copy = remote(
            q_all.at[source], q_all.at[source], q_send.at[at], q_recv.at[at], {"ma": twin}
        )
        copy.start()
        q_to_x.append(copy)
    for copy in q_to_x:
        copy.wait_recv()

    held = q_lead.shape[0]
    lead = remote(
        q_all.at[pl.ds(nma - held, held)], q_lead, lead_sem.at[0], lead_sem.at[1], {"pb": pb + 1}
    )

    @pl.when(has_down)
    def _():
        lead.start()

    for i in range(pair - 1):
        m_to_row[i, order[-1]].start()

    @pl.when(pb == 0)
    def _():
        q_lead[...] = jnp.zeros_like(q_lead)

    @pl.when(ma == 0)
    def _():
        left[...] = jnp.zeros_like(left)

    @pl.when(ma == nma - 1)
    def _():
        right[...] = jnp.zeros_like(right)

    def flat(ref):
        count, each, width = ref.shape
        if each % 16 == 0:
            return ref[...].reshape(count * each, width)
        return ref[...].astype(jnp.float32).reshape(count * each, width).astype(ref.dtype)

    q_count = nma * q_all.shape[1]
    bands = ((LEAD, q_count), (0, LEAD))

    def halo(number, begin, width, into, where):
        rows = pl.ds(*bands[number % 2])
        return remote(
            scores.at[rows, pl.ds(begin, width)],
            into.at[rows],
            halo_send.at[number],
            halo_recv.at[number],
            {"ma": where},
        )

    to_right = [halo(i, m_count - LEFT, LEFT, left, ma + 1) for i in (0, 1)]
    to_left = [halo(i, 0, RIGHT, right, ma - 1) for i in (2, 3)]
    right_part = set(range(m_count - LEFT, m_count, LANES))
    left_part = set(range(0, RIGHT, LANES))

    def score(queries, at, chunk):
        k = m_ref.shape[1]
        block = flat(queries)
        total = None
        for slot in range(npb):
            part = lax.dot_general(
                block[:, slot * k : (slot + 1) * k],
                m_all[slot, pl.ds(chunk * step, step), :],
                (((1,), (1,)), ((), ())),
                preferred_element_type=jnp.float32,
            )
            total = part if total is None else total + part
        scores[pl.ds(at, block.shape[0]), pl.ds(chunk * step, step)] = total

    def send(test, copy):
        @pl.when(test)
        def _():
            copy.start()

    done, sent = set(), set()
    for number, chunk in enumerate(order):
        if number == chunks - 1:

            @pl.when(has_up)
            def _():
                lead.wait_recv()

            for known in order[:-1]:
                score(q_lead, 0, known)
            assert right_part <= done and left_part <= done
            send(has_right, to_right[1])
            send(has_left, to_left[1])
        for i, source in enumerate(rows_from):
            m_to_row[i, chunk].wait_recv()
            at = (pair + i) * chunks + chunk
            m_to_mate[i, chunk] = remote(
                piece(source, chunk), piece(source, chunk), m_send.at[at], m_recv.at[at], {"pb": mate}
            )
            m_to_mate[i, chunk].start()
        for i in range(-1, pair - 1):
            m_to_mate[i, chunk].wait_recv()
        score(q_all, LEAD, chunk)
        done.update(range(chunk * step, (chunk + 1) * step, LANES))
        if right_part <= done and "right" not in sent:
            sent.add("right")
            send(has_right, to_right[0])
        if left_part <= done and "left" not in sent:
            sent.add("left")
            send(has_left, to_left[0])
    score(q_lead, 0, order[-1])

    out_ref[:, pl.ds(LEFT, m_count)] = scores[...]

    @pl.when(has_left)
    def _():
        for copy in to_right:
            copy.wait_recv()

    out_ref[:, pl.ds(0, LEFT)] = left[...]

    @pl.when(has_right)
    def _():
        for copy in to_left:
            copy.wait_recv()

    out_ref[:, pl.ds(LEFT + m_count, RIGHT)] = right[...]

    for copy in q_to_z + q_to_x + list(m_to_row.values()) + list(m_to_mate.values()):
        copy.wait_send()

    @pl.when(has_down)
    def _():
        lead.wait_send()

    @pl.when(has_right)
    def _():
        for copy in to_right:
            copy.wait_send()

    @pl.when(has_left)
    def _():
        for copy in to_left:
            copy.wait_send()


def score_tile(queries, map_descriptors, npb, nma):
    each, width = queries.shape[1:]
    m_count, k = map_descriptors.shape
    q_count = each * nma
    chunks = 4
    held = LEAD // each
    pair, across = npb // CORES, nma // 2
    dma = pltpu.SemaphoreType.DMA
    return pl.pallas_call(
        lambda *refs: score_kernel(npb, nma, chunks, *refs),
        out_shape=jax.ShapeDtypeStruct(
            (LEAD + q_count, LEFT + m_count + RIGHT), jnp.float32
        ),
        in_specs=[pl.BlockSpec(memory_space=pl.ANY)] * 2,
        out_specs=pl.BlockSpec(memory_space=pltpu.VMEM),
        scratch_shapes=[
            pltpu.VMEM((nma, each, width), jnp.bfloat16),
            pltpu.VMEM((held, each, width), jnp.bfloat16),
            pltpu.VMEM((npb, m_count, k), jnp.bfloat16),
            pltpu.VMEM((LEAD + q_count, m_count), jnp.float32),
            pltpu.VMEM((LEAD + q_count, LEFT), jnp.float32),
            pltpu.VMEM((LEAD + q_count, RIGHT), jnp.float32),
            dma((2,)),
            dma((2 * across,)),
            dma((2 * across,)),
            dma((2,)),
            dma((2 * pair * chunks,)),
            dma((2 * pair * chunks,)),
            dma((4,)),
            dma((4,)),
        ],
        compiler_params=pltpu.CompilerParams(
            collective_id=0, has_side_effects=True, vmem_limit_bytes=48 << 20
        ),
        name="scores",
    )(queries, map_descriptors)


def best_kernel(slopes_ref, ext_ref, out_ref, c_ref, a2_ref, a4_ref, a8_ref):
    pb, ma = lax.axis_index("pb"), lax.axis_index("ma")
    rows, width = ext_ref.shape
    q_count, m_count = rows - LEAD, width - LEFT - RIGHT
    halo = LEFT // LANES
    tiles = halo + m_count // LANES
    size = 2 * RAD + 1

    block = 2 * LANES

    def band_of(depth, width, lead):
        inner = lax.broadcasted_iota(jnp.int32, (depth, width), 0)
        outer = lax.broadcasted_iota(jnp.int32, (depth, width), 1)
        near = jnp.abs(inner - lead - outer) <= RAD
        return jnp.where(near, 1.0, 0.0).astype(jnp.bfloat16)

    def window(value, band):
        total = None
        for _ in range(3):
            part = value.astype(jnp.bfloat16)
            value = value - part.astype(jnp.float32)
            term = jnp.dot(part, band, preferred_element_type=jnp.float32)
            total = term if total is None else total + term
        return total * (1.0 / size)

    group = 96
    first_row = jnp.where(pb == 0, LEAD, 0)
    first_col = jnp.where(ma == 0, LEFT, 0)
    edge = band_of(block, LANES, 0)
    inside = band_of(2 * block, block, LANES)

    def contrast(at, tile, lead, count, band):
        begin = tile * LANES - lead
        value = ext_ref[pl.ds(at, group), pl.ds(begin, band.shape[0])]
        centre = value[:, lead : lead + count * LANES]
        average = window(value, band)
        spread = window(value * value, band) - average * average
        normal = (centre - average) * (
            lax.rsqrt(spread + 1.0) * (1.0 / math.sqrt(SEQ))
        )
        row = lax.broadcasted_iota(jnp.int32, normal.shape, 0) + at
        col = lax.broadcasted_iota(jnp.int32, normal.shape, 1) + tile * LANES
        seen = (row >= first_row) & (col >= first_col)
        normal = jnp.where(seen, normal, 0.0)
        for half in range(count):
            c_ref[tile + half, pl.ds(at, group), :] = normal[
                :, half * LANES : (half + 1) * LANES
            ]

    @pl.loop(0, rows // group)
    def _(number):
        at = pl.multiple_of(number * group, 8)
        contrast(at, 0, 0, 1, edge)
        for tile in range(1, tiles, 2):
            contrast(at, tile, LANES, 2, inside)

    out_ref[0] = jnp.full((q_count, m_count), -jnp.inf, jnp.float32)

    def moved(ref, tile, at, count, shift, lane, before):
        here = pltpu.roll(ref[tile, pl.ds(at, count), :], shift, 1)
        return here, jnp.where(lane < shift, here if before is None else before, here)

    def add(dst, src, lag, shift, base, start, count, low):
        lane = lax.broadcasted_iota(jnp.int32, (count, LANES), 1)
        for first in range(start, rows, count):
            at = base + first
            before = None
            if low > 0:
                before = pltpu.roll(src[low - 1, pl.ds(at - lag, count), :], shift, 1)
            for tile in range(low, tiles):
                before, other = moved(src, tile, at - lag, count, shift, lane, before)
                dst[tile, pl.ds(at, count), :] = src[tile, pl.ds(at, count), :] + other

    @pl.loop(0, slopes_ref.shape[0])
    def _(index):
        v = slopes_ref[index]
        base = pl.multiple_of((v // 16) * 8, 8)
        add(a2_ref, c_ref, 1, v, base, 8, 40, 0)
        add(a4_ref, a2_ref, 2, 2 * v, base, 16, 16, halo - 2)
        add(a8_ref, a4_ref, 4, 4 * v, base, 24, 24, halo - 1)
        far = 16 * v
        back, rest = far // LANES, far % LANES
        count = 16
        lane = lax.broadcasted_iota(jnp.int32, (count, LANES), 1)
        for first in range(0, q_count, count):
            at = base + (LEAD + first)
            low = halo - 1
            before8 = pltpu.roll(a8_ref[low, pl.ds(at - 8, count), :], 8 * v, 1)
            before4 = pltpu.roll(a4_ref[low - back, pl.ds(at - 16, count), :], rest, 1)
            for tile in range(halo, tiles):
                before8, eight = moved(a8_ref, tile, at - 8, count, 8 * v, lane, before8)
                before4, four = moved(a4_ref, tile - back, at - 16, count, rest, lane, before4)
                total = a8_ref[tile, pl.ds(at, count), :] + eight + four
                cols = pl.ds((tile - halo) * LANES, LANES)
                out_ref[0, pl.ds(first, count), cols] = jnp.maximum(
                    out_ref[0, pl.ds(first, count), cols], total
                )


def sequence_best(extended, slopes):
    rows, width = extended.shape
    m_count = width - LEFT - RIGHT
    tiles = (LEFT + m_count) // LANES
    return pl.pallas_call(
        best_kernel,
        out_shape=jax.ShapeDtypeStruct((1, rows - LEAD, m_count), jnp.float32),
        in_specs=[
            pl.BlockSpec(memory_space=pltpu.SMEM),
            pl.BlockSpec(memory_space=pltpu.VMEM),
        ],
        out_specs=pl.BlockSpec(memory_space=pltpu.VMEM),
        scratch_shapes=[pltpu.VMEM((tiles, rows, LANES), jnp.float32)] * 4,
        compiler_params=pltpu.CompilerParams(vmem_limit_bytes=32 << 20),
        name="best",
    )(slopes, extended)


def solution(mesh):
    npb, nma = mesh.shape["pb"], mesh.shape["ma"]

    def local(queries, map_descriptors, slopes):
        return sequence_best(score_tile(queries, map_descriptors, npb, nma), slopes)

    return jax.shard_map(
        local,
        mesh=mesh,
        in_specs=(P(None, ("pb", "ma"), None), P("ma", "pb"), P()),
        out_specs=P(None, "pb", "ma"),
        check_vma=False,
    )
```

```python
import math

import jax
import jax.numpy as jnp
from jax import lax
from jax.experimental import pallas as pl
from jax.experimental.pallas import tpu as pltpu
from jax.sharding import PartitionSpec as P

MESH = pl.DeviceIdType.MESH
SEQ = 20
RAD = 10
LEAD = 32
LEFT = 384
RIGHT = 128
LANES = 128
CORES = 2


def remote(src, dst, send, recv, where):
    return pltpu.make_async_remote_copy(
        src_ref=src,
        dst_ref=dst,
        send_sem=send,
        recv_sem=recv,
        device_id=where,
        device_id_type=MESH,
    )


def score_kernel(
    npb,
    nma,
    chunks,
    q_ref,
    m_ref,
    out_ref,
    q_all,
    q_lead,
    m_all,
    scores,
    left,
    right,
    local_sem,
    q_send,
    q_recv,
    lead_sem,
    m_send,
    m_recv,
    halo_send,
    halo_recv,
):
    pb, ma = lax.axis_index("pb"), lax.axis_index("ma")
    pair, across = npb // CORES, nma // 2
    row, core = pb // CORES, pb % CORES
    z, x = ma // 2, ma % 2
    mate = row * CORES + 1 - core
    twin = z * 2 + 1 - x
    rows_other = [((row + i) % pair) * CORES + core for i in range(1, pair)]
    rows_from = [((row + pair - i) % pair) * CORES + core for i in range(1, pair)]
    z_other = [((z + i) % across) * 2 + x for i in range(1, across)]
    z_from = [((z + across - i) % across) * 2 + x for i in range(1, across)]
    has_up, has_down = pb > 0, pb < npb - 1
    has_left, has_right = ma > 0, ma < nma - 1

    load_q = pltpu.make_async_copy(q_ref.at[0], q_all.at[ma], local_sem.at[0])
    load_q.start()
    load_m = pltpu.make_async_copy(m_ref, m_all.at[pb], local_sem.at[1])
    load_m.start()

    barrier = pltpu.get_barrier_semaphore()

    def greet(where):
        pl.semaphore_signal(barrier, inc=1, device_id=where, device_id_type=MESH)

    greet({"pb": mate})
    greet({"ma": twin})
    for other in rows_other:
        greet({"pb": other})
    for other in z_other:
        greet({"ma": other})
    for test, where in (
        (has_up, {"pb": pb - 1}),
        (has_down, {"pb": pb + 1}),
        (has_left, {"ma": ma - 1}),
        (has_right, {"ma": ma + 1}),
    ):

        @pl.when(test)
        def _():
            greet(where)

    edges = sum(
        jnp.where(test, 1, 0) for test in (has_up, has_down, has_left, has_right)
    )
    pl.semaphore_wait(barrier, pair + across + edges)

    load_q.wait()
    q_to_z = [
        remote(q_all.at[ma], q_all.at[ma], q_send.at[i], q_recv.at[i], {"ma": other})
        for i, other in enumerate(z_other)
    ]
    for copy in q_to_z:
        copy.start()
    first = across - 1
    q_to_x = [
        remote(
            q_all.at[ma], q_all.at[ma], q_send.at[first], q_recv.at[first], {"ma": twin}
        )
    ]
    q_to_x[0].start()

    load_m.wait()
    m_count = m_ref.shape[0]
    step = m_count // chunks
    order = list(range(chunks - 1, chunks // 2 - 1, -1)) + list(range(chunks // 2))

    def piece(slot, chunk):
        return m_all.at[slot, pl.ds(chunk * step, step)]

    m_to_row, m_to_mate = {}, {}
    for chunk in order:
        for i, other in enumerate(rows_other):
            at = i * chunks + chunk
            m_to_row[i, chunk] = remote(
                piece(pb, chunk), piece(pb, chunk), m_send.at[at], m_recv.at[at], {"pb": other}
            )
            if chunk != order[-1]:
                m_to_row[i, chunk].start()
    for chunk in order:
        at = (pair - 1) * chunks + chunk
        m_to_mate[-1, chunk] = remote(
            piece(pb, chunk), piece(pb, chunk), m_send.at[at], m_recv.at[at], {"pb": mate}
        )
        m_to_mate[-1, chunk].start()

    for i, source in enumerate(z_from):
        q_to_z[i].wait_recv()
        at = across + i
        copy = remote(
            q_all.at[source], q_all.at[source], q_send.at[at], q_recv.at[at], {"ma": twin}
        )
        copy.start()
        q_to_x.append(copy)
    for copy in q_to_x:
        copy.wait_recv()

    held = q_lead.shape[0]
    lead = remote(
        q_all.at[pl.ds(nma - held, held)], q_lead, lead_sem.at[0], lead_sem.at[1], {"pb": pb + 1}
    )

    @pl.when(has_down)
    def _():
        lead.start()

    for i in range(pair - 1):
        m_to_row[i, order[-1]].start()

    @pl.when(pb == 0)
    def _():
        q_lead[...] = jnp.zeros_like(q_lead)

    @pl.when(ma == 0)
    def _():
        left[...] = jnp.zeros_like(left)

    @pl.when(ma == nma - 1)
    def _():
        right[...] = jnp.zeros_like(right)

    def flat(ref):
        count, each, width = ref.shape
        if each % 16 == 0:
            return ref[...].reshape(count * each, width)
        return ref[...].astype(jnp.float32).reshape(count * each, width).astype(ref.dtype)

    q_count = nma * q_all.shape[1]
    bands = ((LEAD, q_count), (0, LEAD))

    def halo(number, begin, width, into, where):
        rows = pl.ds(*bands[number % 2])
        return remote(
            scores.at[rows, pl.ds(begin, width)],
            into.at[rows],
            halo_send.at[number],
            halo_recv.at[number],
            {"ma": where},
        )

    to_right = [halo(i, m_count - LEFT, LEFT, left, ma + 1) for i in (0, 1)]
    to_left = [halo(i, 0, RIGHT, right, ma - 1) for i in (2, 3)]
    right_part = set(range(m_count - LEFT, m_count, LANES))
    left_part = set(range(0, RIGHT, LANES))

    def score(queries, at, chunk):
        k = m_ref.shape[1]
        block = flat(queries)
        total = None
        for slot in range(npb):
            part = lax.dot_general(
                block[:, slot * k : (slot + 1) * k],
                m_all[slot, pl.ds(chunk * step, step), :],
                (((1,), (1,)), ((), ())),
                preferred_element_type=jnp.float32,
            )
            total = part if total is None else total + part
        scores[pl.ds(at, block.shape[0]), pl.ds(chunk * step, step)] = total
        out_ref[pl.ds(at, block.shape[0]), pl.ds(LEFT + chunk * step, step)] = total

    def send(test, copy):
        @pl.when(test)
        def _():
            copy.start()

    done, sent = set(), set()
    for number, chunk in enumerate(order):
        if number == chunks - 1:

            @pl.when(has_up)
            def _():
                lead.wait_recv()

            for known in order[:-1]:
                score(q_lead, 0, known)
            assert right_part <= done and left_part <= done
            send(has_right, to_right[1])
            send(has_left, to_left[1])
        for i, source in enumerate(rows_from):
            m_to_row[i, chunk].wait_recv()
            at = (pair + i) * chunks + chunk
            m_to_mate[i, chunk] = remote(
                piece(source, chunk), piece(source, chunk), m_send.at[at], m_recv.at[at], {"pb": mate}
            )
            m_to_mate[i, chunk].start()
        for i in range(-1, pair - 1):
            m_to_mate[i, chunk].wait_recv()
        score(q_all, LEAD, chunk)
        done.update(range(chunk * step, (chunk + 1) * step, LANES))
        if right_part <= done and "right" not in sent:
            sent.add("right")
            send(has_right, to_right[0])
        if left_part <= done and "left" not in sent:
            sent.add("left")
            send(has_left, to_left[0])
    score(q_lead, 0, order[-1])


    @pl.when(has_left)
    def _():
        for copy in to_right:
            copy.wait_recv()

    out_ref[:, pl.ds(0, LEFT)] = left[...]

    @pl.when(has_right)
    def _():
        for copy in to_left:
            copy.wait_recv()

    out_ref[:, pl.ds(LEFT + m_count, RIGHT)] = right[...]

    for copy in q_to_z + q_to_x + list(m_to_row.values()) + list(m_to_mate.values()):
        copy.wait_send()

    @pl.when(has_down)
    def _():
        lead.wait_send()

    @pl.when(has_right)
    def _():
        for copy in to_right:
            copy.wait_send()

    @pl.when(has_left)
    def _():
        for copy in to_left:
            copy.wait_send()


def score_tile(queries, map_descriptors, npb, nma):
    each, width = queries.shape[1:]
    m_count, k = map_descriptors.shape
    q_count = each * nma
    chunks = 8
    held = LEAD // each
    pair, across = npb // CORES, nma // 2
    dma = pltpu.SemaphoreType.DMA
    return pl.pallas_call(
        lambda *refs: score_kernel(npb, nma, chunks, *refs),
        out_shape=jax.ShapeDtypeStruct(
            (LEAD + q_count, LEFT + m_count + RIGHT), jnp.float32
        ),
        in_specs=[pl.BlockSpec(memory_space=pl.ANY)] * 2,
        out_specs=pl.BlockSpec(memory_space=pltpu.VMEM),
        scratch_shapes=[
            pltpu.VMEM((nma, each, width), jnp.bfloat16),
            pltpu.VMEM((held, each, width), jnp.bfloat16),
            pltpu.VMEM((npb, m_count, k), jnp.bfloat16),
            pltpu.VMEM((LEAD + q_count, m_count), jnp.float32),
            pltpu.VMEM((LEAD + q_count, LEFT), jnp.float32),
            pltpu.VMEM((LEAD + q_count, RIGHT), jnp.float32),
            dma((2,)),
            dma((2 * across,)),
            dma((2 * across,)),
            dma((2,)),
            dma((2 * pair * chunks,)),
            dma((2 * pair * chunks,)),
            dma((4,)),
            dma((4,)),
        ],
        compiler_params=pltpu.CompilerParams(
            collective_id=0, has_side_effects=True, vmem_limit_bytes=48 << 20
        ),
        name="scores",
    )(queries, map_descriptors)


def best_kernel(slopes_ref, ext_ref, out_ref, c_ref, a2_ref, a4_ref, a8_ref):
    pb, ma = lax.axis_index("pb"), lax.axis_index("ma")
    rows, width = ext_ref.shape
    q_count, m_count = rows - LEAD, width - LEFT - RIGHT
    halo = LEFT // LANES
    tiles = halo + m_count // LANES
    size = 2 * RAD + 1

    block = 2 * LANES

    def band_of(depth, width, lead):
        inner = lax.broadcasted_iota(jnp.int32, (depth, width), 0)
        outer = lax.broadcasted_iota(jnp.int32, (depth, width), 1)
        near = jnp.abs(inner - lead - outer) <= RAD
        return jnp.where(near, 1.0, 0.0).astype(jnp.bfloat16)

    def window(value, band):
        total = None
        for _ in range(3):
            part = value.astype(jnp.bfloat16)
            value = value - part.astype(jnp.float32)
            term = jnp.dot(part, band, preferred_element_type=jnp.float32)
            total = term if total is None else total + term
        return total * (1.0 / size)

    group = 96
    first_row = jnp.where(pb == 0, LEAD, 0)
    first_col = jnp.where(ma == 0, LEFT, 0)
    edge = band_of(block, LANES, 0)
    inside = band_of(2 * block, block, LANES)

    def contrast(at, tile, lead, count, band):
        begin = tile * LANES - lead
        value = ext_ref[pl.ds(at, group), pl.ds(begin, band.shape[0])]
        centre = value[:, lead : lead + count * LANES]
        average = window(value, band)
        spread = window(value * value, band) - average * average
        normal = (centre - average) * (
            lax.rsqrt(spread + 1.0) * (1.0 / math.sqrt(SEQ))
        )
        row = lax.broadcasted_iota(jnp.int32, normal.shape, 0) + at
        col = lax.broadcasted_iota(jnp.int32, normal.shape, 1) + tile * LANES
        seen = (row >= first_row) & (col >= first_col)
        normal = jnp.where(seen, normal, 0.0)
        for half in range(count):
            c_ref[tile + half, pl.ds(at, group), :] = normal[
                :, half * LANES : (half + 1) * LANES
            ]

    @pl.loop(0, rows // group)
    def _(number):
        at = pl.multiple_of(number * group, 8)
        contrast(at, 0, 0, 1, edge)
        for tile in range(1, tiles, 2):
            contrast(at, tile, LANES, 2, inside)

    out_ref[0] = jnp.full((q_count, m_count), -jnp.inf, jnp.float32)

    def moved(ref, tile, at, count, shift, lane, before):
        here = pltpu.roll(ref[tile, pl.ds(at, count), :], shift, 1)
        return here, jnp.where(lane < shift, here if before is None else before, here)

    def add(dst, src, lag, shift, base, start, count, low):
        lane = lax.broadcasted_iota(jnp.int32, (count, LANES), 1)
        for first in range(start, rows, count):
            at = base + first
            before = None
            if low > 0:
                before = pltpu.roll(src[low - 1, pl.ds(at - lag, count), :], shift, 1)
            for tile in range(low, tiles):
                before, other = moved(src, tile, at - lag, count, shift, lane, before)
                dst[tile, pl.ds(at, count), :] = src[tile, pl.ds(at, count), :] + other

    @pl.loop(0, slopes_ref.shape[0])
    def _(index):
        v = slopes_ref[index]
        base = pl.multiple_of((v // 16) * 8, 8)
        add(a2_ref, c_ref, 1, v, base, 8, 40, 0)
        add(a4_ref, a2_ref, 2, 2 * v, base, 16, 16, halo - 2)
        add(a8_ref, a4_ref, 4, 4 * v, base, 24, 24, halo - 1)
        far = 16 * v
        back, rest = far // LANES, far % LANES
        count = 16
        lane = lax.broadcasted_iota(jnp.int32, (count, LANES), 1)
        for first in range(0, q_count, count):
            at = base + (LEAD + first)
            low = halo - 1
            before8 = pltpu.roll(a8_ref[low, pl.ds(at - 8, count), :], 8 * v, 1)
            before4 = pltpu.roll(a4_ref[low - back, pl.ds(at - 16, count), :], rest, 1)
            for tile in range(halo, tiles):
                before8, eight = moved(a8_ref, tile, at - 8, count, 8 * v, lane, before8)
                before4, four = moved(a4_ref, tile - back, at - 16, count, rest, lane, before4)
                total = a8_ref[tile, pl.ds(at, count), :] + eight + four
                cols = pl.ds((tile - halo) * LANES, LANES)
                out_ref[0, pl.ds(first, count), cols] = jnp.maximum(
                    out_ref[0, pl.ds(first, count), cols], total
                )


def sequence_best(extended, slopes):
    rows, width = extended.shape
    m_count = width - LEFT - RIGHT
    tiles = (LEFT + m_count) // LANES
    return pl.pallas_call(
        best_kernel,
        out_shape=jax.ShapeDtypeStruct((1, rows - LEAD, m_count), jnp.float32),
        in_specs=[
            pl.BlockSpec(memory_space=pltpu.SMEM),
            pl.BlockSpec(memory_space=pltpu.VMEM),
        ],
        out_specs=pl.BlockSpec(memory_space=pltpu.VMEM),
        scratch_shapes=[pltpu.VMEM((tiles, rows, LANES), jnp.float32)] * 4,
        compiler_params=pltpu.CompilerParams(vmem_limit_bytes=32 << 20),
        name="best",
    )(slopes, extended)


def solution(mesh):
    npb, nma = mesh.shape["pb"], mesh.shape["ma"]

    def local(queries, map_descriptors, slopes):
        return sequence_best(score_tile(queries, map_descriptors, npb, nma), slopes)

    return jax.shard_map(
        local,
        mesh=mesh,
        in_specs=(P(None, ("pb", "ma"), None), P("ma", "pb"), P()),
        out_specs=P(None, "pb", "ma"),
        check_vma=False,
    )
```

```python
import math

import jax
import jax.numpy as jnp
from jax import lax
from jax.experimental import pallas as pl
from jax.experimental.pallas import tpu as pltpu
from jax.sharding import PartitionSpec as P

MESH = pl.DeviceIdType.MESH
SEQ = 20
RAD = 10
LEAD = 32
LEFT = 384
RIGHT = 128
LANES = 128
CORES = 2


def remote(src, dst, send, recv, where):
    return pltpu.make_async_remote_copy(
        src_ref=src,
        dst_ref=dst,
        send_sem=send,
        recv_sem=recv,
        device_id=where,
        device_id_type=MESH,
    )


def score_kernel(
    npb,
    nma,
    chunks,
    q_ref,
    m_ref,
    out_ref,
    q_all,
    q_lead,
    m_all,
    scores,
    left,
    right,
    local_sem,
    q_send,
    q_recv,
    lead_sem,
    m_send,
    m_recv,
    halo_send,
    halo_recv,
):
    pb, ma = lax.axis_index("pb"), lax.axis_index("ma")
    pair, across = npb // CORES, nma // 2
    row, core = pb // CORES, pb % CORES
    z, x = ma // 2, ma % 2
    mate = row * CORES + 1 - core
    twin = z * 2 + 1 - x
    rows_other = [((row + i) % pair) * CORES + core for i in range(1, pair)]
    rows_from = [((row + pair - i) % pair) * CORES + core for i in range(1, pair)]
    z_other = [((z + i) % across) * 2 + x for i in range(1, across)]
    z_from = [((z + across - i) % across) * 2 + x for i in range(1, across)]
    has_up, has_down = pb > 0, pb < npb - 1
    has_left, has_right = ma > 0, ma < nma - 1

    load_q = pltpu.make_async_copy(q_ref.at[0], q_all.at[ma], local_sem.at[0])
    load_q.start()
    load_m = pltpu.make_async_copy(m_ref, m_all.at[pb], local_sem.at[1])
    load_m.start()

    barrier = pltpu.get_barrier_semaphore()

    def greet(where):
        pl.semaphore_signal(barrier, inc=1, device_id=where, device_id_type=MESH)

    greet({"pb": mate})
    greet({"ma": twin})
    for other in rows_other:
        greet({"pb": other})
    for other in z_other:
        greet({"ma": other})
    for test, where in (
        (has_up, {"pb": pb - 1}),
        (has_down, {"pb": pb + 1}),
        (has_left, {"ma": ma - 1}),
        (has_right, {"ma": ma + 1}),
    ):

        @pl.when(test)
        def _():
            greet(where)

    edges = sum(
        jnp.where(test, 1, 0) for test in (has_up, has_down, has_left, has_right)
    )
    pl.semaphore_wait(barrier, pair + across + edges)

    load_q.wait()
    q_to_z = [
        remote(q_all.at[ma], q_all.at[ma], q_send.at[i], q_recv.at[i], {"ma": other})
        for i, other in enumerate(z_other)
    ]
    for copy in q_to_z:
        copy.start()
    first = across - 1
    q_to_x = [
        remote(
            q_all.at[ma], q_all.at[ma], q_send.at[first], q_recv.at[first], {"ma": twin}
        )
    ]
    q_to_x[0].start()

    load_m.wait()
    m_count = m_ref.shape[0]
    step = m_count // chunks
    order = list(range(chunks - 1, chunks // 2 - 1, -1)) + list(range(chunks // 2))

    def piece(slot, chunk):
        return m_all.at[slot, pl.ds(chunk * step, step)]

    m_to_row, m_to_mate = {}, {}
    for chunk in order:
        for i, other in enumerate(rows_other):
            at = i * chunks + chunk
            m_to_row[i, chunk] = remote(
                piece(pb, chunk), piece(pb, chunk), m_send.at[at], m_recv.at[at], {"pb": other}
            )
            if chunk != order[-1]:
                m_to_row[i, chunk].start()
    for chunk in order:
        at = (pair - 1) * chunks + chunk
        m_to_mate[-1, chunk] = remote(
            piece(pb, chunk), piece(pb, chunk), m_send.at[at], m_recv.at[at], {"pb": mate}
        )
        m_to_mate[-1, chunk].start()

    for i, source in enumerate(z_from):
        q_to_z[i].wait_recv()
        at = across + i
        copy = remote(
            q_all.at[source], q_all.at[source], q_send.at[at], q_recv.at[at], {"ma": twin}
        )
        copy.start()
        q_to_x.append(copy)
    for copy in q_to_x:
        copy.wait_recv()

    held = q_lead.shape[0]
    lead = remote(
        q_all.at[pl.ds(nma - held, held)], q_lead, lead_sem.at[0], lead_sem.at[1], {"pb": pb + 1}
    )

    @pl.when(has_down)
    def _():
        lead.start()

    for i in range(pair - 1):
        m_to_row[i, order[-1]].start()

    @pl.when(pb == 0)
    def _():
        q_lead[...] = jnp.zeros_like(q_lead)

    @pl.when(ma == 0)
    def _():
        left[...] = jnp.zeros_like(left)

    @pl.when(ma == nma - 1)
    def _():
        right[...] = jnp.zeros_like(right)

    def flat(ref):
        count, each, width = ref.shape
        if each % 16 == 0:
            return ref[...].reshape(count * each, width)
        return ref[...].astype(jnp.float32).reshape(count * each, width).astype(ref.dtype)

    q_count = nma * q_all.shape[1]
    bands = ((LEAD, q_count), (0, LEAD))

    def halo(number, begin, width, into, where):
        rows = pl.ds(*bands[number % 2])
        return remote(
            scores.at[rows, pl.ds(begin, width)],
            into.at[rows],
            halo_send.at[number],
            halo_recv.at[number],
            {"ma": where},
        )

    to_right = [halo(i, m_count - LEFT, LEFT, left, ma + 1) for i in (0, 1)]
    to_left = [halo(i, 0, RIGHT, right, ma - 1) for i in (2, 3)]
    right_part = set(range(m_count - LEFT, m_count, LANES))
    left_part = set(range(0, RIGHT, LANES))

    def score(queries, at, chunk):
        k = m_ref.shape[1]
        block = flat(queries)
        total = None
        for slot in range(npb):
            part = lax.dot_general(
                block[:, slot * k : (slot + 1) * k],
                m_all[slot, pl.ds(chunk * step, step), :],
                (((1,), (1,)), ((), ())),
                preferred_element_type=jnp.float32,
            )
            total = part if total is None else total + part
        scores[pl.ds(at, block.shape[0]), pl.ds(chunk * step, step)] = total
        out_ref[pl.ds(at, block.shape[0]), pl.ds(LEFT + chunk * step, step)] = total

    def send(test, copy):
        @pl.when(test)
        def _():
            copy.start()

    done, sent = set(), set()
    for number, chunk in enumerate(order):
        if number == chunks - 1:

            @pl.when(has_up)
            def _():
                lead.wait_recv()

            for known in order[:-1]:
                score(q_lead, 0, known)
            assert right_part <= done and left_part <= done
            send(has_right, to_right[1])
            send(has_left, to_left[1])
        for i, source in enumerate(rows_from):
            m_to_row[i, chunk].wait_recv()
            at = (pair + i) * chunks + chunk
            m_to_mate[i, chunk] = remote(
                piece(source, chunk), piece(source, chunk), m_send.at[at], m_recv.at[at], {"pb": mate}
            )
            m_to_mate[i, chunk].start()
        for i in range(-1, pair - 1):
            m_to_mate[i, chunk].wait_recv()
        score(q_all, LEAD, chunk)
        done.update(range(chunk * step, (chunk + 1) * step, LANES))
        if right_part <= done and "right" not in sent:
            sent.add("right")
            send(has_right, to_right[0])
        if left_part <= done and "left" not in sent:
            sent.add("left")
            send(has_left, to_left[0])
    score(q_lead, 0, order[-1])


    @pl.when(has_left)
    def _():
        for copy in to_right:
            copy.wait_recv()

    out_ref[:, pl.ds(0, LEFT)] = left[...]

    @pl.when(has_right)
    def _():
        for copy in to_left:
            copy.wait_recv()

    out_ref[:, pl.ds(LEFT + m_count, RIGHT)] = right[...]

    for copy in q_to_z + q_to_x + list(m_to_row.values()) + list(m_to_mate.values()):
        copy.wait_send()

    @pl.when(has_down)
    def _():
        lead.wait_send()

    @pl.when(has_right)
    def _():
        for copy in to_right:
            copy.wait_send()

    @pl.when(has_left)
    def _():
        for copy in to_left:
            copy.wait_send()


def score_tile(queries, map_descriptors, npb, nma):
    each, width = queries.shape[1:]
    m_count, k = map_descriptors.shape
    q_count = each * nma
    chunks = 4
    held = LEAD // each
    pair, across = npb // CORES, nma // 2
    dma = pltpu.SemaphoreType.DMA
    return pl.pallas_call(
        lambda *refs: score_kernel(npb, nma, chunks, *refs),
        out_shape=jax.ShapeDtypeStruct(
            (LEAD + q_count, LEFT + m_count + RIGHT), jnp.float32
        ),
        in_specs=[pl.BlockSpec(memory_space=pl.ANY)] * 2,
        out_specs=pl.BlockSpec(memory_space=pltpu.VMEM),
        scratch_shapes=[
            pltpu.VMEM((nma, each, width), jnp.bfloat16),
            pltpu.VMEM((held, each, width), jnp.bfloat16),
            pltpu.VMEM((npb, m_count, k), jnp.bfloat16),
            pltpu.VMEM((LEAD + q_count, m_count), jnp.float32),
            pltpu.VMEM((LEAD + q_count, LEFT), jnp.float32),
            pltpu.VMEM((LEAD + q_count, RIGHT), jnp.float32),
            dma((2,)),
            dma((2 * across,)),
            dma((2 * across,)),
            dma((2,)),
            dma((2 * pair * chunks,)),
            dma((2 * pair * chunks,)),
            dma((4,)),
            dma((4,)),
        ],
        compiler_params=pltpu.CompilerParams(
            collective_id=0, has_side_effects=True, vmem_limit_bytes=48 << 20
        ),
        name="scores",
    )(queries, map_descriptors)


def best_kernel(slopes_ref, ext_ref, out_ref, c_ref, a2_ref, a4_ref, a8_ref):
    pb, ma = lax.axis_index("pb"), lax.axis_index("ma")
    rows, width = ext_ref.shape
    q_count, m_count = rows - LEAD, width - LEFT - RIGHT
    halo = LEFT // LANES
    tiles = halo + m_count // LANES
    size = 2 * RAD + 1

    block = 2 * LANES

    def band_of(depth, width, lead):
        inner = lax.broadcasted_iota(jnp.int32, (depth, width), 0)
        outer = lax.broadcasted_iota(jnp.int32, (depth, width), 1)
        near = jnp.abs(inner - lead - outer) <= RAD
        return jnp.where(near, 1.0, 0.0).astype(jnp.bfloat16)

    def window(value, band):
        total = None
        for _ in range(3):
            part = value.astype(jnp.bfloat16)
            value = value - part.astype(jnp.float32)
            term = jnp.dot(part, band, preferred_element_type=jnp.float32)
            total = term if total is None else total + term
        return total * (1.0 / size)

    group = 96
    first_row = jnp.where(pb == 0, LEAD, 0)
    first_col = jnp.where(ma == 0, LEFT, 0)
    edge = band_of(block, LANES, 0)
    inside = band_of(2 * block, block, LANES)

    def contrast(at, tile, lead, count, band):
        begin = tile * LANES - lead
        value = ext_ref[pl.ds(at, group), pl.ds(begin, band.shape[0])]
        centre = value[:, lead : lead + count * LANES]
        average = window(value, band)
        spread = window(value * value, band) - average * average
        normal = (centre - average) * (
            lax.rsqrt(spread + 1.0) * (1.0 / math.sqrt(SEQ))
        )
        row = lax.broadcasted_iota(jnp.int32, normal.shape, 0) + at
        col = lax.broadcasted_iota(jnp.int32, normal.shape, 1) + tile * LANES
        seen = (row >= first_row) & (col >= first_col)
        normal = jnp.where(seen, normal, 0.0)
        for half in range(count):
            c_ref[tile + half, pl.ds(at, group), :] = normal[
                :, half * LANES : (half + 1) * LANES
            ]

    @pl.loop(0, rows // group)
    def _(number):
        at = pl.multiple_of(number * group, 8)
        contrast(at, 0, 0, 1, edge)
        for tile in range(1, tiles, 2):
            contrast(at, tile, LANES, 2, inside)

    out_ref[0] = jnp.full((q_count, m_count), -jnp.inf, jnp.float32)

    def moved(ref, tile, at, count, shift, lane, before):
        here = pltpu.roll(ref[tile, pl.ds(at, count), :], shift, 1)
        return here, jnp.where(lane < shift, here if before is None else before, here)

    def add(dst, src, lag, shift, base, start, count, low):
        lane = lax.broadcasted_iota(jnp.int32, (count, LANES), 1)
        for first in range(start, rows, count):
            at = base + first
            before = None
            if low > 0:
                before = pltpu.roll(src[low - 1, pl.ds(at - lag, count), :], shift, 1)
            for tile in range(low, tiles):
                before, other = moved(src, tile, at - lag, count, shift, lane, before)
                dst[tile, pl.ds(at, count), :] = src[tile, pl.ds(at, count), :] + other

    @pl.loop(0, slopes_ref.shape[0])
    def _(index):
        v = slopes_ref[index]
        base = pl.multiple_of((v // 16) * 8, 8)
        add(a2_ref, c_ref, 1, v, base, 8, 40, 0)
        add(a4_ref, a2_ref, 2, 2 * v, base, 16, 16, halo - 2)
        add(a8_ref, a4_ref, 4, 4 * v, base, 24, 24, halo - 1)
        far = 16 * v
        back, rest = far // LANES, far % LANES
        count = 16
        lane = lax.broadcasted_iota(jnp.int32, (count, LANES), 1)
        for first in range(0, q_count, count):
            at = base + (LEAD + first)
            low = halo - 1
            before8 = pltpu.roll(a8_ref[low, pl.ds(at - 8, count), :], 8 * v, 1)
            before4 = pltpu.roll(a4_ref[low - back, pl.ds(at - 16, count), :], rest, 1)
            for tile in range(halo, tiles):
                before8, eight = moved(a8_ref, tile, at - 8, count, 8 * v, lane, before8)
                before4, four = moved(a4_ref, tile - back, at - 16, count, rest, lane, before4)
                total = a8_ref[tile, pl.ds(at, count), :] + eight + four
                cols = pl.ds((tile - halo) * LANES, LANES)
                out_ref[0, pl.ds(first, count), cols] = jnp.maximum(
                    out_ref[0, pl.ds(first, count), cols], total
                )


def sequence_best(extended, slopes):
    rows, width = extended.shape
    m_count = width - LEFT - RIGHT
    tiles = (LEFT + m_count) // LANES
    return pl.pallas_call(
        best_kernel,
        out_shape=jax.ShapeDtypeStruct((1, rows - LEAD, m_count), jnp.float32),
        in_specs=[
            pl.BlockSpec(memory_space=pltpu.SMEM),
            pl.BlockSpec(memory_space=pltpu.VMEM),
        ],
        out_specs=pl.BlockSpec(memory_space=pltpu.VMEM),
        scratch_shapes=[pltpu.VMEM((tiles, rows, LANES), jnp.float32)] * 4,
        compiler_params=pltpu.CompilerParams(vmem_limit_bytes=32 << 20),
        name="best",
    )(slopes, extended)


def solution(mesh):
    npb, nma = mesh.shape["pb"], mesh.shape["ma"]

    def local(queries, map_descriptors, slopes):
        return sequence_best(score_tile(queries, map_descriptors, npb, nma), slopes)

    return jax.shard_map(
        local,
        mesh=mesh,
        in_specs=(P(None, ("pb", "ma"), None), P("ma", "pb"), P()),
        out_specs=P(None, "pb", "ma"),
        check_vma=False,
    )
```
